256 devices in a mesh: inst: 8 (over z_hi, y), space: 32 (over z_lo, x, core).
Axes of the slice: x: 4, y: 4, z: 8 (z_hi: 2, z_lo: 4; z = z_hi * 4 + z_lo), core: 2. Of those that a mesh axis runs over, the one named last changes fastest.
Arguments:
- flow_state: float32 [16, 4, 192, 8, 512], P('inst', None, 'space'), may hold values from -6 to 6
- radial_first: float32 [512, 512], replicated, may hold values from -0.25 to 0.25
- radial_second: float32 [512, 512], replicated, may hold values from -0.25 to 0.25
- radial_flow: float32 [192, 512], P('space'), may hold values from -6 to 6
- swirl_flow: float32 [512, 192], replicated, may hold values from -6 to 6
- radius_inverse: float32 [512], replicated, may hold values from 0.05 to 1
- radial_flux: float32 [4, 4], replicated, may hold values from -3 to 3
- swirl_flux: float32 [4, 4], replicated, may hold values from -3 to 3
- cross_flux: float32 [4, 4], replicated, may hold values from -3 to 3
- span_flux: float32 [4, 4], replicated, may hold values from -3 to 3
- frequency: float32 [1], replicated, may hold values from 0.5 to 1.5
- viscosity: float32 [1], replicated, may hold values from 0.05 to 0.3
Outputs:
- residual: float32 [16, 4, 192, 8, 512], P('inst', None, 'space')
The draws below stay inside these ranges and needn't reach their ends.
All inputs are finite; a program needn't handle non-finite values.
Results may differ from the reference program's by a relative error of at most 0.000055.
Values sent between devices are 32-bit elements; how exact they have to be, the bound alone decides.
No kernel may reach another device: no remote copies, remote signals or barrier semaphores. Data moves between devices by JAX's collectives and lax.ppermute only.
A program may use at most 64 MiB of HBM per device.

```python
import math
import jax
import jax.numpy as jnp
from jax import lax

RADIAL = 512
AZIMUTH = 192
VARS = 4
PLANES = 8
INSTANCES = 16


def block_levels(rng, dims, shards, least, top_value):
    level, own = 1.0, jax.random.fold_in(rng, 6)
    for axis_at, parts in shards:
        steps = jnp.exp(jax.random.uniform(jax.random.fold_in(own, axis_at), (parts,), jnp.float32, least / len(shards), top_value / len(shards)))
        level = level * jnp.repeat(steps, dims[axis_at] // parts).reshape([-1 if axis == axis_at else 1 for axis in range(len(dims))])
    return level


def gaussian(own_key, extent, scale, bound, pieces=(), dtype=jnp.bfloat16):
    level = block_levels(own_key, extent, pieces, -0.22, 0.18) if pieces else 1.0
    drawn = jax.random.normal(own_key, extent, jnp.float32) * scale * level
    return jnp.minimum(jnp.maximum(drawn, -bound), bound).astype(dtype)


def setup_inputs(seed: int = 0) -> dict:
    key_of = jax.random.split(jax.random.key(seed), 13)
    return {
        "flow_state": gaussian(key_of[0], (INSTANCES, VARS, AZIMUTH, PLANES, RADIAL), 1.0, 6.0, ((0, 8), (2, 32)), jnp.float32),
        "radial_first": gaussian(key_of[1], (RADIAL, RADIAL), RADIAL ** -0.5, 0.25, (), jnp.float32),
        "radial_second": gaussian(key_of[2], (RADIAL, RADIAL), RADIAL ** -0.5, 0.25, (), jnp.float32),
        "radial_flow": gaussian(key_of[3], (AZIMUTH, RADIAL), 1.0, 6.0, ((0, 32),), jnp.float32),
        "swirl_flow": gaussian(key_of[4], (RADIAL, AZIMUTH), 1.0, 6.0, (), jnp.float32),
        "radius_inverse": jnp.clip(jnp.exp(jax.random.uniform(key_of[5], (RADIAL,), jnp.float32, math.log(0.05), math.log(1.0))), 0.05, 1.0),
        "radial_flux": gaussian(key_of[6], (VARS, VARS), VARS ** -0.5, 3.0, (), jnp.float32),
        "swirl_flux": gaussian(key_of[7], (VARS, VARS), VARS ** -0.5, 3.0, (), jnp.float32),
        "cross_flux": gaussian(key_of[8], (VARS, VARS), VARS ** -0.5, 3.0, (), jnp.float32),
        "span_flux": gaussian(key_of[9], (VARS, VARS), VARS ** -0.5, 3.0, (), jnp.float32),
        "frequency": jnp.clip(jax.random.uniform(key_of[10], (1,), jnp.float32, 0.5, 1.5), 0.5, 1.5),
        "viscosity": jnp.clip(jax.random.uniform(key_of[11], (1,), jnp.float32, 0.05, 0.3), 0.05, 0.3),
    }


highest = lax.Precision.HIGHEST


def spectral(points):
    indices = jnp.arange(points)
    offsets = (indices[:, None] - indices[None, :]) % points
    spacing = 2.0 * math.pi / points
    angles = offsets.astype(jnp.float32) * (math.pi / points)
    parity = (1 - 2 * (offsets % 2)).astype(jnp.float32)
    nonzero = offsets != 0
    sines = jnp.where(nonzero, jnp.sin(angles), jnp.float32(1.0))
    first = jnp.where(nonzero, 0.5 * parity * jnp.cos(angles) / sines, jnp.float32(0.0))
    diagonal_value = -math.pi ** 2 / (3.0 * spacing ** 2) - 1.0 / 6.0
    second = jnp.where(nonzero, -0.5 * parity / (sines * sines), jnp.float32(diagonal_value))
    return first, second


def apply_flux(matrix, fields):
    return jnp.einsum('uv,v...->u...', matrix, fields, precision=highest)


def reference(flow_state, radial_first, radial_second, radial_flow, swirl_flow, radius_inverse, radial_flux, swirl_flux, cross_flux, span_flux, frequency, viscosity):
    time_matrix, unused = spectral(INSTANCES)
    turn_first, turn_second = spectral(AZIMUTH)
    spacing = 2.0 * math.pi / AZIMUTH
    turn_first = spacing * turn_first
    turn_second = (spacing * spacing) * turn_second
    coupled = frequency[0] * jnp.einsum('nm,mvtzr->nvtzr', time_matrix, flow_state, precision=highest)
    swirl_coeff = (swirl_flow.T * radius_inverse[None, :])[:, None, :]
    radial_coeff = radial_flow[:, None, :]
    viscous = viscosity[0]

    def one_instance(fields):
        radial_slope = jnp.einsum('vtzs,rs->vtzr', fields, radial_first, precision=highest)
        radial_curve = jnp.einsum('vtzs,rs->vtzr', fields, radial_second, precision=highest)
        turn_slope = jnp.einsum('st,vtzr->vszr', turn_first, fields, precision=highest)
        turn_curve = jnp.einsum('st,vtzr->vszr', turn_second, fields, precision=highest)
        cross_slope = jnp.einsum('st,vtzr->vszr', turn_first, radial_slope, precision=highest)
        upper = jnp.roll(fields, -1, axis=2)
        lower = jnp.roll(fields, 1, axis=2)
        span_slope = 0.5 * (upper - lower)
        span_curve = upper + lower - 2.0 * fields
        turning = swirl_coeff * turn_slope + radius_inverse * apply_flux(swirl_flux, turn_slope)
        turning = turning + radius_inverse * apply_flux(cross_flux, cross_slope)
        turning = turning - viscous * (radius_inverse * radius_inverse) * turn_curve
        radial_part = radial_coeff * radial_slope + apply_flux(radial_flux, radial_slope)
        radial_part = radial_part - viscous * (radial_curve + radius_inverse * radial_slope)
        radial_part = radial_part + apply_flux(span_flux, span_slope) - viscous * span_curve
        return turning + radial_part

    return coupled + lax.map(one_instance, flow_state)
```

```python
import functools
import math

import jax
import jax.numpy as jnp
import numpy as np
from jax import lax
from jax.experimental import pallas as pl
from jax.experimental.pallas import tpu as pltpu
from jax.sharding import PartitionSpec as P

F32, BF16 = jnp.float32, jnp.bfloat16


def spectral(points):
    indices = np.arange(points)
    offsets = (indices[:, None] - indices[None, :]) % points
    spacing = 2.0 * math.pi / points
    angles = offsets * (math.pi / points)
    parity = 1.0 - 2.0 * (offsets % 2)
    nonzero = offsets != 0
    sines = np.where(nonzero, np.sin(angles), 1.0)
    first = np.where(nonzero, 0.5 * parity * np.cos(angles) / sines, 0.0)
    diagonal_value = -math.pi**2 / (3.0 * spacing**2) - 1.0 / 6.0
    second = np.where(nonzero, -0.5 * parity / (sines * sines), diagonal_value)
    return first, second


def halves(x):
    high = x.astype(BF16)
    return high, (x - high.astype(F32)).astype(BF16)


def product(a, b, dims):
    dot = functools.partial(
        lax.dot_general, dimension_numbers=(dims, ((), ())), preferred_element_type=F32
    )
    return dot(a[0], b[0]) + (dot(a[0], b[1]) + dot(a[1], b[0]))


ROWS = ((1,), (0,))
LINES = ((1,), (1,))


LANES = 128


def pack_kernel(*refs, planes, rows, parts):
    *tiles, x_ref, lines_ref, times_ref = refs
    for t, tile in enumerate(tiles):
        for z in range(planes):
            lines_ref[z, t // 2, t % 2] = tile[0, pl.ds(z, rows, stride=planes), :]
    chunk = x_ref.shape[1] // parts
    for j in range(parts):
        times_ref[j, 0] = x_ref[0, pl.ds(j * chunk, chunk), :]


def radial_kernel(
    x_ref, r1_ref, r2_ref, flow_ref, q_ref, kr_ref, ks_ref, nu_ref, out_ref, s1h, s1l, s2h, s2l
):
    @pl.when(pl.program_id(0) == 0)
    def _():
        s1h[...], s1l[...] = halves(r1_ref[...])
        s2h[...], s2l[...] = halves(r2_ref[...])

    nu = nu_ref[0]
    variables, count = x_ref.shape[1], x_ref.shape[2]
    planes, radial = x_ref.shape[3], x_ref.shape[4]
    rows = count * planes
    r1, r2 = (s1h[...], s1l[...]), (s2h[...], s2l[...])
    q = q_ref[...].reshape(1, 1, radial)
    flow = flow_ref[...].reshape(count, 1, radial)
    slopes, spans, bases = [], [], []
    for v in range(variables):
        field = x_ref[0, v]
        parts = halves(field.reshape(rows, radial))
        slope = product(parts, r1, LINES).reshape(count, planes, radial)
        curve = product(parts, r2, LINES).reshape(count, planes, radial)
        upper = jnp.roll(field, -1, axis=1)
        lower = jnp.roll(field, 1, axis=1)
        slopes.append(slope)
        spans.append(0.5 * (upper - lower))
        bases.append(flow * slope - nu * (curve + q * slope + (upper + lower - 2.0 * field)))
    for u in range(variables):
        total = bases[u]
        for v in range(variables):
            total = total + kr_ref[u, v] * slopes[v] + ks_ref[u, v] * spans[v]
        out_ref[0, u] = total


def turn_kernel(
    own_ref,
    other_ref,
    d1h,
    d1l,
    d2h,
    d2l,
    roh,
    rol,
    rph,
    rpl,
    swirl_ref,
    q_ref,
    kw_ref,
    kc_ref,
    nu_ref,
    out_ref,
    slope_s,
    cross_s,
    base_s,
    *,
    variables,
    count,
    sources,
):
    nu = nu_ref[0]
    stride = variables * count
    q = q_ref[...]
    d1, d2 = (d1h[...], d1l[...]), (d2h[...], d2l[...])
    r_own, r_other = (roh[...], rol[...]), (rph[...], rpl[...])

    def lines(ref, v):
        return jnp.concatenate(
            [
                jnp.concatenate(
                    [
                        ref[pl.ds(t * stride + v * count + a, sources, stride=2 * stride), :]
                        for a in range(count)
                    ],
                    0,
                )
                for t in range(2)
            ],
            1,
        )

    swirl = swirl_ref[...]
    for v in range(variables):
        own = halves(lines(own_ref, v))
        other = halves(lines(other_ref, v))
        radial = product(own, r_own, LINES) + product(other, r_other, LINES)
        slope = product(d1, own, ROWS)
        curve = product(d2, own, ROWS)
        slope_s[v] = slope
        cross_s[v] = product(d1, halves(radial), ROWS)
        base_s[v] = q * (swirl * slope - (nu * q) * curve)
    for a in range(count):
        at = pl.ds(a * sources, sources)
        for u in range(variables):
            mixed = kw_ref[u, 0] * slope_s[0, at, :] + kc_ref[u, 0] * cross_s[0, at, :]
            for v in range(1, variables):
                mixed = mixed + kw_ref[u, v] * slope_s[v, at, :] + kc_ref[u, v] * cross_s[v, at, :]
            total = base_s[u, at, :] + q * mixed
            for t in range(2):
                rows = pl.ds(t * stride + u * count + a, sources, stride=2 * stride)
                out_ref[rows, :] = total[:, t * LANES : (t + 1) * LANES]


def time_kernel(x_ref, freq_ref, out_ref, *, matrix):
    points, rows = x_ref.shape[0], x_ref.shape[1]
    step = 8
    freq = freq_ref[0]
    for r in range(0, rows, step):
        at = pl.ds(r, step)
        values = [x_ref[m, at, :] for m in range(points)]
        for n in range(points):
            total = None
            for m in range(points):
                if matrix[n, m] != 0.0:
                    term = float(matrix[n, m]) * values[m]
                    total = term if total is None else total + term
            out_ref[n, at, :] = freq * total


def sum_kernel(radial_ref, times_ref, lines_ref, out_ref, spread, *, planes, rows, parts):
    chunk = out_ref.shape[1] // parts
    for t in range(spread.shape[0]):
        lanes = pl.ds(t * LANES, LANES)
        for z in range(planes):
            spread[t, pl.ds(z, rows, stride=planes), :] = lines_ref[z, t // 2, t % 2]
        for j in range(parts):
            at = pl.ds(j * chunk, chunk)
            out_ref[0, at, lanes] = (
                radial_ref[0, at, lanes] + times_ref[j, 0, :, lanes] + spread[t, at, :]
            )


def vmem():
    return pl.BlockSpec(memory_space=pltpu.VMEM)


def smem():
    return pl.BlockSpec(memory_space=pltpu.SMEM)


def on_device(
    flow_state,
    radial_first,
    radial_second,
    radial_flow,
    swirl_flow,
    radius_inverse,
    radial_flux,
    swirl_flux,
    cross_flux,
    span_flux,
    frequency,
    viscosity,
):
    inst, variables, count, planes, radial = flow_state.shape
    n_inst = lax.axis_size("inst")
    n_space = lax.axis_size("space")
    azimuth = n_space * count
    half = radial // 2
    rows = variables * count
    lines = rows * planes
    instances = inst * n_inst
    cells = lines // n_inst
    assert inst * planes * 2 == n_space and lines % (8 * n_inst) == 0 and radial == 4 * LANES

    time_matrix, _ = spectral(instances)
    turn_first, turn_second = spectral(azimuth)
    spacing = 2.0 * math.pi / azimuth
    order = np.arange(azimuth).reshape(n_space, count).T.reshape(-1)
    turns = []
    for matrix, scale in ((turn_first, spacing), (turn_second, spacing * spacing)):
        matrix = jnp.asarray((scale * matrix)[np.ix_(order, order)].astype(np.float32))
        turns.extend(halves(matrix))

    state = flow_state.reshape(inst, lines, radial)
    tiles = radial // LANES
    to_lines, to_times = pl.pallas_call(
        functools.partial(pack_kernel, planes=planes, rows=rows, parts=n_inst),
        grid=(inst,),
        in_specs=[
            pl.BlockSpec((1, lines, LANES), lambda i, t=t: (i, 0, t)) for t in range(tiles)
        ]
        + [pl.BlockSpec((1, lines, radial), lambda i: (i, 0, 0))],
        out_specs=[
            pl.BlockSpec((planes, 2, 2, rows, LANES), lambda i: (i, 0, 0, 0, 0)),
            pl.BlockSpec((n_inst, 1, cells, radial), lambda i: (0, i, 0, 0)),
        ],
        out_shape=[
            jax.ShapeDtypeStruct((inst * planes, 2, 2, rows, LANES), F32),
            jax.ShapeDtypeStruct((n_inst, inst, cells, radial), F32),
        ],
        name="pack",
    )(*[state] * (tiles + 1))
    to_lines = to_lines.reshape(n_space, 2 * rows, LANES)

    own = lax.all_to_all(to_lines, "space", 0, 0, tiled=True)
    other = lax.ppermute(own, "space", [(i, i ^ 1) for i in range(n_space)])

    core = lax.rem(lax.axis_index("space"), 2)
    mine = lax.dynamic_slice(radial_first, (core * half, 0), (half, radial))
    r_own = halves(lax.dynamic_slice(mine, (0, core * half), (half, half)))
    r_other = halves(lax.dynamic_slice(mine, (0, (1 - core) * half), (half, half)))
    q_mine = lax.dynamic_slice(radius_inverse, (core * half,), (half,)).reshape(1, half)
    swirl = lax.dynamic_slice(swirl_flow.T, (0, core * half), (azimuth, half))
    swirl = swirl.reshape(n_space, count, half).swapaxes(0, 1).reshape(azimuth, half)

    turned = pl.pallas_call(
        functools.partial(turn_kernel, variables=variables, count=count, sources=n_space),
        in_specs=[vmem()] * 12 + [smem()] * 3,
        out_specs=vmem(),
        out_shape=jax.ShapeDtypeStruct((n_space * 2 * rows, LANES), F32),
        scratch_shapes=[pltpu.VMEM((variables, azimuth, half), F32)] * 3,
        name="turn",
    )(
        own.reshape(n_space * 2 * rows, LANES),
        other.reshape(n_space * 2 * rows, LANES),
        *turns,
        *r_own,
        *r_other,
        swirl,
        q_mine,
        swirl_flux,
        cross_flux,
        viscosity,
    )
    turned = lax.all_to_all(
        turned.reshape(n_space, 2 * rows, LANES), "space", 0, 0, tiled=True
    ).reshape(inst * planes, 2, 2, rows, LANES)

    times = lax.all_to_all(to_times, "inst", 0, 0, tiled=True)
    coupled = pl.pallas_call(
        functools.partial(time_kernel, matrix=time_matrix.astype(np.float32)),
        in_specs=[vmem(), smem()],
        out_specs=vmem(),
        out_shape=jax.ShapeDtypeStruct((instances, cells, radial), F32),
        name="times",
    )(times.reshape(instances, cells, radial), frequency)
    coupled = lax.all_to_all(
        coupled.reshape(n_inst, inst, cells, radial), "inst", 0, 0, tiled=True
    )

    whole = lambda *shape: pl.BlockSpec(shape, lambda i: (0,) * len(shape))
    radial_part = pl.pallas_call(
        radial_kernel,
        grid=(inst,),
        in_specs=[
            pl.BlockSpec((1, variables, count, planes, radial), lambda i: (i, 0, 0, 0, 0)),
            whole(radial, radial),
            whole(radial, radial),
            whole(count, radial),
            whole(1, radial),
            smem(),
            smem(),
            smem(),
        ],
        out_specs=pl.BlockSpec((1, variables, count, planes, radial), lambda i: (i, 0, 0, 0, 0)),
        out_shape=jax.ShapeDtypeStruct(flow_state.shape, F32),
        scratch_shapes=[pltpu.VMEM((radial, radial), BF16)] * 4,
        name="radial",
    )(
        flow_state,
        radial_first,
        radial_second,
        radial_flow,
        radius_inverse.reshape(1, radial),
        radial_flux,
        span_flux,
        viscosity,
    )

    total = pl.pallas_call(
        functools.partial(sum_kernel, planes=planes, rows=rows, parts=n_inst),
        grid=(inst,),
        in_specs=[
            pl.BlockSpec((1, lines, radial), lambda i: (i, 0, 0)),
            pl.BlockSpec((n_inst, 1, cells, radial), lambda i: (0, i, 0, 0)),
            pl.BlockSpec((planes, 2, 2, rows, LANES), lambda i: (i, 0, 0, 0, 0)),
        ],
        out_specs=pl.BlockSpec((1, lines, radial), lambda i: (i, 0, 0)),
        scratch_shapes=[pltpu.VMEM((tiles, lines, LANES), F32)],
        out_shape=jax.ShapeDtypeStruct((inst, lines, radial), F32),
        name="sum",
    )(radial_part.reshape(inst, lines, radial), coupled, turned)
    return total.reshape(flow_state.shape)


def solution(mesh):
    in_specs = (
        P("inst", None, "space", None, None),
        P(),
        P(),
        P("space", None),
        P(),
        P(),
        P(),
        P(),
        P(),
        P(),
        P(),
        P(),
    )
    out_specs = P("inst", None, "space", None, None)
    return jax.shard_map(
        on_device, mesh=mesh, in_specs=in_specs, out_specs=out_specs, check_vma=False
    )
```
